128 devices in a mesh: dom: 128 (over y, x, z, core).
Axes of the slice: x: 4, y: 4, z: 4, core: 2. Of those that a mesh axis runs over, the one named last changes fastest.
Arguments:
- coefficients: float32 [56, 9, 32768], P(None, None, 'dom'), may hold values from -6 to 6
- star_matrices: float32 [3, 9, 9, 32768], P(None, None, None, 'dom'), may hold values from -3 to 3
- own_flux: float32 [9, 9, 4, 32768], P(None, None, None, 'dom'), may hold values from -2 to 2
- neighbour_flux: float32 [9, 9, 4, 32768], P(None, None, None, 'dom'), may hold values from -2 to 2
- stiffness: float32 [3, 56, 56], replicated, may hold values from -0.75 to 0.75
- projection: float32 [4, 21, 56], replicated, may hold values from -0.75 to 0.75
- rotation: float32 [3, 21, 21], replicated, may hold values from -1.25 to 1.25
- fault_minus: float32 [9, 9, 16384], P(None, None, 'dom'), may hold values from -2 to 2
- fault_plus: float32 [9, 9, 16384], P(None, None, 'dom'), may hold values from -2 to 2
- slip_compliance: float32 [16384], P('dom'), may hold values from 0.1 to 10
- neighbour_slot: int32 [4, 32768], P(None, 'dom'), may hold values from 0 to 767, as said below
- neighbour_code: int32 [4, 32768], P(None, 'dom'), may hold values from 0 to 11, as said below
- halo_send: int32 [4, 16384], P(None, 'dom'), may hold values from 0 to 1023, as said below
- fault_table: int32 [3, 16384], P(None, 'dom'), may hold values from -1 to 1023, as said below
Outputs:
- next_coefficients: float32 [56, 9, 32768], P(None, None, 'dom')
The draws below stay inside these ranges and needn't reach their ends.
Inputs may be any that keep to these rules, and one draw needn't show every extreme that they name: `neighbour_slot`: A value of 256 or more names a received halo slot as in the reference program; faces listed in fault_table take their state from the fault instead. `neighbour_code`: 3 j + h; for a face whose slot is 256 or more, j equals the matching halo_send entry // 256. `halo_send`: row o, slot s of a device: j * 256 + e, face j of its element e, whose data go to the device at index plus shift[o] (shift = 1, 2, -1, -2, cyclic). `fault_table`: exactly a quarter of the devices own fault faces, drawn from the seed; a device's columns c * 1 to c + 1 - 1 hold its faces for owner c, all filled if c owns and -1, -1, 0 if not; the faces named on one device all differ.
All inputs are finite; a program needn't handle non-finite values.
Results may differ from the reference program's by a relative error of at most 0.0003.
Values sent between devices are 32-bit elements; how exact they have to be, the bound alone decides.
No kernel may reach another device: no remote copies, remote signals or barrier semaphores. Data moves between devices by JAX's collectives and lax.ppermute only.
A program may use at most 192 MiB of HBM per device.

```python
import math
import jax
import jax.numpy as jnp
from jax import lax

BASIS = 56
QUANTITIES = 9
FACE_BASIS = 21
ORDER = 6
DIRS = 3
FACES = 4
E_DEV = 256
HALO_SLOTS = 128
FAULT_CAP = 1
ELEMS = 32768
FLT_DEV = 128
FAULTS = 16384
N_DOM = 128


SHIFTS = (1, 2, -1, -2)


def halo_tables(key):
    send_ids = jax.random.randint(jax.random.fold_in(key, 101), (4, HALO_SLOTS * N_DOM), 0, 4 * E_DEV, dtype=jnp.int32)
    slot_ids = jax.random.randint(jax.random.fold_in(key, 102), (4, E_DEV * N_DOM), 0, E_DEV + 4 * HALO_SLOTS, dtype=jnp.int32)
    local_faces = jax.random.randint(jax.random.fold_in(key, 103), (4, E_DEV * N_DOM), 0, 4, dtype=jnp.int32)
    turn_codes = jax.random.randint(jax.random.fold_in(key, 104), (4, E_DEV * N_DOM), 0, 3, dtype=jnp.int32)
    device = (jnp.arange(E_DEV * N_DOM, dtype=jnp.int32) // E_DEV)[None, :]
    remote = slot_ids - E_DEV
    offset_index = jnp.clip(remote // HALO_SLOTS, 0, 3)
    position = remote % HALO_SLOTS
    shifts = jnp.array(SHIFTS, dtype=jnp.int32)
    source = (device - shifts[offset_index]) % N_DOM
    sent_entry = send_ids[offset_index, source * HALO_SLOTS + position]
    faces = jnp.where(slot_ids >= E_DEV, sent_entry // E_DEV, local_faces)
    return (send_ids, slot_ids, faces * 3 + turn_codes)


def draw_halo_send(key, part):
    return halo_tables(key)[0]


def draw_neighbour_slot(key, part):
    return halo_tables(key)[1]


def draw_neighbour_code(key, part):
    return halo_tables(key)[2]


def draw_fault_table(key, part):
    ordering = jax.random.permutation(jax.random.fold_in(key, 201), N_DOM)
    owner_flag = jnp.zeros((N_DOM,), jnp.int32).at[ordering[:N_DOM // 4]].set(1)
    fault_column = jnp.arange(FLT_DEV, dtype=jnp.int32)
    active = owner_flag[fault_column // FAULT_CAP] > 0
    ranking = jnp.where(active, jnp.cumsum(active.astype(jnp.int32)) - 1, 0)
    face_key = jax.random.fold_in(key, 202)

    def per_device(device):
        picks = jax.random.permutation(jax.random.fold_in(face_key, device), 4 * E_DEV).astype(jnp.int32)
        return (picks[2 * ranking], picks[2 * ranking + 1])
    minus_face, plus_face = jax.vmap(per_device)(jnp.arange(N_DOM, dtype=jnp.int32))
    turn_codes = jax.random.randint(jax.random.fold_in(key, 203), (N_DOM, FLT_DEV), 0, 3, dtype=jnp.int32)
    minus_face = jnp.where(active[None, :], minus_face, -1)
    plus_face = jnp.where(active[None, :], plus_face, -1)
    turn_codes = jnp.where(active[None, :], turn_codes, 0)
    return jnp.stack([minus_face, plus_face, turn_codes]).reshape(3, N_DOM * FLT_DEV)


def levels(own_key, extent, cuts, least, high):
    factor_of, own = 1.0, jax.random.fold_in(own_key, 6)
    for axis_at, parts in cuts:
        steps = jnp.exp(jax.random.uniform(jax.random.fold_in(own, axis_at), (parts,), jnp.float32, least / len(cuts), high / len(cuts)))
        factor_of = factor_of * jnp.repeat(steps, extent[axis_at] // parts).reshape([-1 if axis == axis_at else 1 for axis in range(len(extent))])
    return factor_of


def centred(key, dims, width, most, split=(), kind=jnp.bfloat16):
    gain = levels(key, dims, split, -0.22, 0.18) if split else 1.0
    drawn = jax.random.normal(key, dims, jnp.float32) * width * gain
    return jnp.minimum(jnp.maximum(drawn, -most), most).astype(kind)


def setup_inputs(seed: int = 0) -> dict:
    keys = jax.random.split(jax.random.key(seed), 15)
    return {
        "coefficients": centred(keys[0], (BASIS, QUANTITIES, ELEMS), 1.0, 6.0, ((2, 128),), jnp.float32),
        "star_matrices": centred(keys[1], (DIRS, QUANTITIES, QUANTITIES, ELEMS), 4 ** -0.5, 3.0, ((3, 128),), jnp.float32),
        "own_flux": centred(keys[2], (QUANTITIES, QUANTITIES, FACES, ELEMS), QUANTITIES ** -0.5, 2.0, ((3, 128),), jnp.float32),
        "neighbour_flux": centred(keys[3], (QUANTITIES, QUANTITIES, FACES, ELEMS), QUANTITIES ** -0.5, 2.0, ((3, 128),), jnp.float32),
        "stiffness": centred(keys[4], (DIRS, BASIS, BASIS), BASIS ** -0.5, 0.75, (), jnp.float32),
        "projection": centred(keys[5], (FACES, FACE_BASIS, BASIS), BASIS ** -0.5, 0.75, (), jnp.float32),
        "rotation": centred(keys[6], (3, FACE_BASIS, FACE_BASIS), FACE_BASIS ** -0.5, 1.25, (), jnp.float32),
        "fault_minus": centred(keys[7], (QUANTITIES, QUANTITIES, FAULTS), QUANTITIES ** -0.5, 2.0, ((2, 128),), jnp.float32),
        "fault_plus": centred(keys[8], (QUANTITIES, QUANTITIES, FAULTS), QUANTITIES ** -0.5, 2.0, ((2, 128),), jnp.float32),
        "slip_compliance": jnp.clip(jnp.exp(math.log(10.0) - 4.6051702 * jax.random.uniform(keys[9], (FAULTS,), jnp.float32) ** levels(keys[9], (FAULTS,), ((0, 128),), -0.2, 0.2)), 0.1, 10.0),
        "neighbour_slot": draw_neighbour_slot(jax.random.fold_in(keys[14], 71), 0),
        "neighbour_code": draw_neighbour_code(jax.random.fold_in(keys[14], 71), 0),
        "halo_send": draw_halo_send(jax.random.fold_in(keys[14], 71), 0),
        "fault_table": draw_fault_table(jax.random.fold_in(keys[14], 71), 0),
    }


PRECISE = lax.Precision.HIGHEST
SHIFTS = (1, 2, -1, -2)


def apply_matrix(matrix, values):
    flattened = values.reshape(values.shape[0], -1)
    product = jnp.dot(matrix, flattened, precision=PRECISE, preferred_element_type=jnp.float32)
    return product.reshape((matrix.shape[0],) + values.shape[1:])


def mix_quantities(values, matrices):
    return jnp.einsum("mpe,pqe->mqe", values, matrices, precision=PRECISE, preferred_element_type=jnp.float32)


def mix_directions(stacked, values, star_block):
    directions = star_block.shape[0]
    applied = apply_matrix(stacked, values)
    applied = applied.reshape((directions, applied.shape[0] // directions) + applied.shape[1:])
    return jnp.einsum("impe,ipqe->mqe", applied, star_block, precision=PRECISE, preferred_element_type=jnp.float32)


def time_integral(coefficients, star_block, stiffness):
    stacked = stiffness.reshape(-1, stiffness.shape[2])
    derivative = coefficients
    integral = coefficients
    factor = 1.0
    for degree in range(1, ORDER):
        following = mix_directions(stacked, derivative, star_block)
        factor = factor / (degree + 1)
        integral = integral + factor * following
        derivative = following
    return integral


def volume_term(integral, star_block, stiffness):
    stacked = jnp.transpose(stiffness, (0, 2, 1)).reshape(-1, stiffness.shape[1])
    return mix_directions(stacked, integral, star_block)


def face_traces(integral, projection):
    return jnp.stack([apply_matrix(projection[face], integral) for face in range(projection.shape[0])], axis=2)


def rotate(values, turn_codes, rotation, backward):
    summed = jnp.zeros_like(values)
    for turn_index in range(rotation.shape[0]):
        matrix = rotation[turn_index].T if backward else rotation[turn_index]
        summed = summed + jnp.where((turn_codes == turn_index)[None, None, :], apply_matrix(matrix, values), 0.0)
    return summed


def friction(near_side, far_side, left_matrix, right_matrix, compliance):
    shear_mask = (jnp.arange(near_side.shape[1]) >= 3)[None, :, None]
    slip_ratio = (compliance / (1.0 + compliance))[None, None, :]
    slip_term = jnp.where(shear_mask, slip_ratio * (far_side - near_side), 0.0)
    minus_flux = mix_quantities(near_side, left_matrix) + mix_quantities(far_side, right_matrix) + slip_term
    plus_flux = mix_quantities(far_side, left_matrix) + mix_quantities(near_side, right_matrix) - slip_term
    return minus_flux, plus_flux


def reference(coefficients, star_matrices, own_flux, neighbour_flux, stiffness, projection, rotation, fault_minus, fault_plus, slip_compliance, neighbour_slot, neighbour_code, halo_send, fault_table):
    elements = E_DEV

    def first_pass(device):
        first_col = device * elements
        block = lax.dynamic_slice_in_dim(coefficients, first_col, elements, 2)
        star_block = lax.dynamic_slice_in_dim(star_matrices, first_col, elements, 3)
        integral = time_integral(block, star_block, stiffness)
        updated = block + volume_term(integral, star_block, stiffness)
        return face_traces(integral, projection), updated

    devices = jnp.arange(N_DOM, dtype=jnp.int32)
    traces_all, updated_all = lax.map(first_pass, devices)
    shifts = jnp.array(SHIFTS, dtype=jnp.int32)

    def second_pass(device):
        first_col = device * elements
        slot_ids = lax.dynamic_slice_in_dim(neighbour_slot, first_col, elements, 1).reshape(-1)
        face_codes = lax.dynamic_slice_in_dim(neighbour_code, first_col, elements, 1).reshape(-1)
        remote = slot_ids - elements
        offset_index = jnp.clip(remote // HALO_SLOTS, 0, 3)
        position = remote % HALO_SLOTS
        source = (device - shifts[offset_index]) % N_DOM
        sent_entry = halo_send[offset_index, source * HALO_SLOTS + position]
        is_remote = slot_ids >= elements
        from_device = jnp.where(is_remote, source, device)
        from_element = jnp.where(is_remote, sent_entry % elements, slot_ids)
        from_face = jnp.where(is_remote, sent_entry // elements, face_codes // 3)
        gathered = traces_all[from_device, :, :, from_face, from_element]
        neighbour = rotate(jnp.transpose(gathered, (1, 2, 0)), face_codes % 3, rotation, False)
        own_block = traces_all[device]
        own_traces = own_block.reshape(own_block.shape[0], own_block.shape[1], 4 * elements)
        quants = own_traces.shape[1]
        own_mats = lax.dynamic_slice_in_dim(own_flux, first_col, elements, 3).reshape(quants, quants, 4 * elements)
        far_mats = lax.dynamic_slice_in_dim(neighbour_flux, first_col, elements, 3).reshape(quants, quants, 4 * elements)
        state = mix_quantities(own_traces, own_mats) + mix_quantities(neighbour, far_mats)
        fault_rows = lax.dynamic_slice_in_dim(fault_table, device * FLT_DEV, FLT_DEV, 1)
        active = fault_rows[0] >= 0
        turn_codes = fault_rows[2]
        fault_column = jnp.arange(FLT_DEV, dtype=jnp.int32)
        global_index = (fault_column // FAULT_CAP) * FLT_DEV + device * FAULT_CAP + fault_column % FAULT_CAP
        left_matrix = fault_minus[:, :, global_index]
        right_matrix = fault_plus[:, :, global_index]
        compliance = slip_compliance[global_index]
        near_side = own_traces[:, :, jnp.where(active, fault_rows[0], 0)]
        far_side = rotate(own_traces[:, :, jnp.where(active, fault_rows[1], 0)], turn_codes, rotation, False)
        minus_flux, plus_flux = friction(near_side, far_side, left_matrix, right_matrix, compliance)
        plus_flux = rotate(plus_flux, turn_codes, rotation, True)
        beyond = 4 * elements
        state = state.at[:, :, jnp.where(active, fault_rows[0], beyond)].set(minus_flux, mode="drop")
        state = state.at[:, :, jnp.where(active, fault_rows[1], beyond)].set(plus_flux, mode="drop")
        lifted = apply_matrix(projection[0].T, state[:, :, 0:elements])
        for face in range(1, projection.shape[0]):
            lifted = lifted + apply_matrix(projection[face].T, state[:, :, face * elements:(face + 1) * elements])
        return updated_all[device] - lifted

    blocks = lax.map(second_pass, devices)
    return jnp.transpose(blocks, (1, 2, 0, 3)).reshape(blocks.shape[1], blocks.shape[2], N_DOM * elements)
```

```python
import functools
import jax
import jax.numpy as jnp
from jax import lax
from jax.experimental import pallas as pl
from jax.experimental.pallas import tpu as pltpu
from jax.sharding import PartitionSpec as P

ORDER = 6
SHIFTS = (1, 2, -1, -2)
F32 = jnp.float32
BF16 = jnp.bfloat16

NB, NQ, NM, NF, NE, NS = 56, 9, 21, 4, 256, 128
MP = 24
BP = 64
RT = NQ * MP
ETA_ROW = 176
PLUS_ROW = 88
GROUPS = ((0, 32), (32, 24))


def split(x):
    hi = x.astype(BF16)
    lo = (x - hi.astype(F32)).astype(BF16)
    return hi, lo


def dot(a, b):
    return jnp.dot(a, b, preferred_element_type=F32)


def dot_t(a, b):
    return lax.dot_general(a, b, (((1,), (1,)), ((), ())), preferred_element_type=F32)


def put_weights(ref, rows, w, width):
    hi, lo = split(w)
    k = w.shape[1]
    ref[rows, 0:k] = hi
    ref[rows, width : width + k] = hi
    ref[rows, 2 * width : 2 * width + k] = lo


def zero_pad_rows(ref):
    zeros = jnp.zeros((BP - NB, NE), BF16)
    for q in range(NQ):
        for part in range(3):
            ref[q, part * BP + NB : (part + 1) * BP, :] = zeros


def put_split(ref, q, row, count, lanes, x):
    hi, lo = split(x)
    ref[q, row : row + count, lanes] = hi
    ref[q, BP + row : BP + row + count, lanes] = hi
    ref[q, 2 * BP + row : 2 * BP + row + count, lanes] = lo


def mix_star(t_ref, star_ref, row, count, lanes):
    acc = [None] * NQ
    for p in range(NQ):
        for i in range(3):
            t = t_ref[p, i * NB + row : i * NB + row + count, lanes]
            for q in range(NQ):
                s = jnp.broadcast_to(star_ref[p, q, i : i + 1, lanes], (count, 128))
                acc[q] = t * s if acc[q] is None else acc[q] + t * s
    return acc


def mix_flux(src_ref, flux_ref, face, lanes):
    acc = [None] * NQ
    for p in range(NQ):
        t = src_ref[face, p * MP : (p + 1) * MP, lanes]
        for q in range(NQ):
            s = jnp.broadcast_to(flux_ref[p, q, face : face + 1, lanes], (MP, 128))
            acc[q] = t * s if acc[q] is None else acc[q] + t * s
    return acc


def half(h):
    return pl.ds(pl.multiple_of(h * 128, 128), 128)


def one_hot(ids, rows, offset):
    row = lax.broadcasted_iota(jnp.int32, (rows, ids.shape[1]), 0) + offset
    return jnp.where(row == ids, 1.0, 0.0).astype(BF16)


def picked(src, hot):
    hi, lo = split(src)
    out = dot(jnp.concatenate([hi, lo], 0), hot)
    return out[: src.shape[0]] + out[src.shape[0] :]


def weights_hhl(ref, rows, w, width):
    hi, lo = split(w)
    k = w.shape[1]
    ref[rows, 0:k] = hi
    ref[rows, width : width + k] = lo
    ref[rows, 2 * width : 2 * width + k] = hi


def pack_kernel(minus_ref, plus_ref, eta_ref, out_ref, scr):
    scr[...] = jnp.zeros_like(scr)
    for p in range(NQ):
        scr[p * NQ : (p + 1) * NQ, :] = minus_ref[p]
        scr[PLUS_ROW + p * NQ : PLUS_ROW + (p + 1) * NQ, :] = plus_ref[p]
    scr[ETA_ROW : ETA_ROW + 1, :] = eta_ref[...]
    out_ref[:, 0, :] = scr[0:128, :].T
    out_ref[:, 1, :] = scr[128:256, :].T


def time_kernel(coef_ref, star_ref, stiff_ref, proj_ref, send_ref, xs_ref, tr_ref, *rest):
    pays, (t_ref, w_ref, int_ref, pw_ref) = rest[:4], rest[4:]
    w_ref[...] = jnp.zeros_like(w_ref)
    pw_ref[...] = jnp.zeros_like(pw_ref)
    for i in range(3):
        weights_hhl(w_ref, slice(i * NB, (i + 1) * NB), stiff_ref[i], BP)
    for f in range(NF):
        weights_hhl(pw_ref, slice(f * MP, f * MP + NM), proj_ref[:, f, :], BP)
    zero_pad_rows(xs_ref)
    for q in range(NQ):
        for row, count in GROUPS:
            x = coef_ref[q, row : row + count, :]
            put_split(xs_ref, q, row, count, slice(0, NE), x)
            int_ref[q, row : row + count, :] = x

    def stage(k, factor):
        factor = factor / (k + 2).astype(F32)
        for q in range(NQ):
            t_ref[q] = dot(w_ref[...], xs_ref[q])

        def by_half(h, c):
            lanes = half(h)
            for row, count in GROUPS:
                acc = mix_star(t_ref, star_ref, row, count, lanes)
                for q in range(NQ):
                    put_split(xs_ref, q, row, count, lanes, acc[q])
                    int_ref[q, row : row + count, lanes] += factor * acc[q]
            return c

        lax.fori_loop(0, 2, by_half, 0)
        return factor

    lax.fori_loop(0, ORDER - 1, stage, jnp.float32(1.0))
    for q in range(NQ):
        for row, count in GROUPS:
            put_split(xs_ref, q, row, count, slice(0, NE), int_ref[q, row : row + count, :])
    for q in range(NQ):
        tr = dot(pw_ref[...], xs_ref[q])
        for f in range(NF):
            tr_ref[f, q * MP : (q + 1) * MP, :] = tr[f * MP : (f + 1) * MP]
    for o in range(0, NF, 2):
        ids = jnp.concatenate([send_ref[o : o + 1, :], send_ref[o + 1 : o + 2, :]], 1)
        acc = None
        for f in range(NF):
            got = picked(tr_ref[f], one_hot(ids, NE, f * NE))
            acc = got if acc is None else acc + got
        pays[o][...] = acc[:, :NS]
        pays[o + 1][...] = acc[:, NS:]


def turned(w_ref, x):
    hi, lo = split(x)
    return dot(w_ref[0], hi) + dot(w_ref[1], hi) + dot(w_ref[0], lo)


def local_kernel(
    coef_ref, xs_ref, tr_ref, star_ref, stiff_ref, proj_ref, rot_ref, own_ref,
    slot_ref, code_ref, table_ref, par_ref,
    part_ref, g_ref, wf_ref, idr_ref,
    t_ref, w_ref, pt_ref, rw_ref, rtw_ref, st_ref, scr, hot_ref, fs_ref,
):
    w_ref[...] = jnp.zeros_like(w_ref)
    for i in range(3):
        weights_hhl(w_ref, slice(i * NB, (i + 1) * NB), stiff_ref[i].T, BP)
    pt_ref[...] = jnp.zeros_like(pt_ref)
    wf_ref[...] = jnp.zeros_like(wf_ref)
    rw_ref[...] = jnp.zeros_like(rw_ref)
    rtw_ref[...] = jnp.zeros_like(rtw_ref)
    for h in range(3):
        hi, lo = split(rot_ref[h])
        rw_ref[0, h * MP : h * MP + NM, 0:NM] = hi
        rw_ref[1, h * MP : h * MP + NM, 0:NM] = lo
        hi, lo = split(rot_ref[h].T)
        rtw_ref[0, h * MP : h * MP + NM, 0:NM] = hi
        rtw_ref[1, h * MP : h * MP + NM, 0:NM] = lo
    for f in range(NF):
        pt = proj_ref[:, f, :].T
        hi, lo = split(pt)
        pt_ref[:, f * MP : f * MP + NM] = hi
        pt_ref[:, 96 + f * MP : 96 + f * MP + NM] = lo
        pt_ref[:, 192 + f * MP : 192 + f * MP + NM] = hi
        for h in range(3):
            rhi, rlo = split(rot_ref[h])
            w = dot(hi, rhi) + dot(lo, rhi) + dot(hi, rlo)
            whi, wlo = split(w)
            at = h * 96 + f * MP
            wf_ref[:, at : at + NM] = whi
            wf_ref[:, 288 + at : 288 + at + NM] = wlo
            wf_ref[:, 576 + at : 576 + at + NM] = whi

    table = table_ref[...]
    active = table[0:1] >= 0
    ids = jnp.concatenate([jnp.where(active, table[0:1], -1), jnp.where(active, table[1:2], -1)], 1)
    turn = table[2:3]
    for f in range(NF):
        hot_ref[f] = one_hot(ids, NE, f * NE)
    pair = None
    for f in range(NF):
        got = picked(tr_ref[f], hot_ref[f])
        pair = got if pair is None else pair + got
    scr[0:128, :] = par_ref[:, 0, :].T
    scr[128:256, :] = par_ref[:, 1, :].T
    eta = scr[ETA_ROW : ETA_ROW + 1, :]
    ratio = eta / (1.0 + eta)
    raw = jnp.concatenate([pair[q * MP : (q + 1) * MP, NS:] for q in range(NQ)], 1)
    tall = turned(rw_ref, raw)

    def choose(tall, q):
        out = jnp.zeros((MP, NS), F32)
        for h in range(3):
            piece = tall[h * MP : (h + 1) * MP, q * NS : (q + 1) * NS]
            out = jnp.where(turn == h, piece, out)
        return out

    near = [pair[q * MP : (q + 1) * MP, :NS] for q in range(NQ)]
    far = [choose(tall, q) for q in range(NQ)]
    minus, plus = [], []
    for q in range(NQ):
        a = b = None
        for p in range(NQ):
            g = jnp.broadcast_to(scr[p * NQ + q : p * NQ + q + 1, :], (MP, NS))
            hh = jnp.broadcast_to(
                scr[PLUS_ROW + p * NQ + q : PLUS_ROW + p * NQ + q + 1, :], (MP, NS)
            )
            x = near[p] * g + far[p] * hh
            y = far[p] * g + near[p] * hh
            a = x if a is None else a + x
            b = y if b is None else b + y
        if q >= 3:
            slip = ratio * (far[q] - near[q])
            a = a + slip
            b = b - slip
        minus.append(a)
        plus.append(b)
    back = turned(rtw_ref, jnp.concatenate(plus, 1))
    for q in range(NQ):
        fs_ref[q * MP : (q + 1) * MP, :NS] = minus[q]
        fs_ref[q * MP : (q + 1) * MP, NS:] = choose(back, q)
    fs_hi, fs_lo = split(fs_ref[...])
    fs2 = jnp.concatenate([fs_hi, fs_lo, jnp.ones((16, NE), BF16)], 0)
    code = code_ref[...]
    slots = slot_ref[...]
    idr_ref[...] = jnp.full_like(idr_ref, -1)
    free = []
    for f in range(NF):
        got = dot_t(fs2, hot_ref[f])
        st_ref[f] = got[:RT] + got[RT : 2 * RT]
        listed = got[2 * RT : 2 * RT + 1] > 0.5
        free.append(jnp.where(listed, 0.0, 1.0))
        slot = slots[f : f + 1]
        remote = slot >= NE
        idr_ref[f : f + 1, :] = jnp.where(remote & ~listed, slot - NE, -1)
        own_id = (code[f : f + 1] // 3) * NE + slot
        own_id = jnp.where(remote | listed, -1, own_id)
        acc = None
        for s in range(NF):
            got = picked(tr_ref[s], one_hot(own_id, NE, s * NE))
            acc = got if acc is None else acc + got
        g_ref[f] = acc
    for f in range(NF):
        for h in range(2):
            lanes = slice(h * 128, (h + 1) * 128)
            acc = mix_flux(tr_ref, own_ref, f, lanes)
            keep = free[f][:, lanes]
            for q in range(NQ):
                rows = slice(q * MP, (q + 1) * MP)
                st_ref[f, rows, lanes] = st_ref[f, rows, lanes] + keep * acc[q]
    for q in range(NQ):
        t_ref[q] = dot(w_ref[...], xs_ref[q])

    def by_half(h, c):
        lanes = half(h)
        for row, count in GROUPS:
            acc = mix_star(t_ref, star_ref, row, count, lanes)
            for q in range(NQ):
                part_ref[q, row : row + count, lanes] = (
                    coef_ref[q, row : row + count, lanes] + acc[q]
                )
        return c

    lax.fori_loop(0, 2, by_half, 0)
    for q in range(NQ):
        state = jnp.concatenate([st_ref[f, q * MP : (q + 1) * MP, :] for f in range(NF)], 0)
        hi, lo = split(state)
        part_ref[q] = part_ref[q] - dot(pt_ref[...], jnp.concatenate([hi, hi, lo], 0))


def far_kernel(
    part_ref, g_ref, wf_ref, idr_ref, far_ref, code_ref, r0, r1, r2, r3, out_ref,
    gs_ref, z_ref, mask_ref,
):
    got_in = (r0, r1, r2, r3)
    code = code_ref[...] % 3
    for f in range(NF):
        for h in range(3):
            row = jnp.broadcast_to(jnp.where(code[f : f + 1] == h, 1.0, 0.0), (MP, NE))
            mask_ref[h, f * MP : (f + 1) * MP, :] = row
    pool = [jnp.concatenate([got_in[o][...], got_in[o + 1][...]], 1) for o in (0, 2)]
    for f in range(NF):
        ids = idr_ref[f : f + 1, :]
        acc = g_ref[f]
        for s in range(2):
            acc = acc + picked(pool[s], one_hot(ids, NE, s * NE))
        gs_ref[f] = acc
    for f in range(NF):
        for h in range(2):
            lanes = slice(h * 128, (h + 1) * 128)
            acc = mix_flux(gs_ref, far_ref, f, lanes)
            for q in range(NQ):
                z_ref[q, f * MP : (f + 1) * MP, lanes] = acc[q]
    masks = [mask_ref[h].astype(BF16) for h in range(3)]
    for q in range(NQ):
        hi, lo = split(z_ref[q])
        his = [hi * m for m in masks]
        los = [lo * m for m in masks]
        out_ref[q] = part_ref[q] - dot(wf_ref[...], jnp.concatenate(his + his + los, 0))


def sds(shape, dtype=F32):
    return jax.ShapeDtypeStruct(shape, dtype)


def shifted(block, distance):
    n = lax.axis_size("dom")
    return lax.ppermute(block, "dom", [((i - distance) % n, i) for i in range(n)])


def call(kernel, out, scratch, name, flops=10**8):
    return pl.pallas_call(
        kernel,
        out_shape=out,
        scratch_shapes=scratch,
        name=name,
        cost_estimate=pl.CostEstimate(flops=flops, bytes_accessed=3 * 10**6, transcendentals=0),
    )


def shards(
    coefficients, star_matrices, own_flux, neighbour_flux, stiffness, projection, rotation,
    fault_minus, fault_plus, slip_compliance, neighbour_slot, neighbour_code, halo_send, fault_table,
):
    coef = jnp.transpose(coefficients, (1, 0, 2))
    star = jnp.transpose(star_matrices, (1, 2, 0, 3))
    proj = jnp.transpose(projection, (1, 0, 2))
    V = pltpu.VMEM
    packed = call(pack_kernel, sds((128, 2, 128)), [V((256, 128), F32)], "pack")(
        fault_minus, fault_plus, slip_compliance.reshape(1, -1)
    )
    params = lax.all_to_all(packed, "dom", 0, 0, tiled=True)
    xs, tr, *pays = call(
        time_kernel,
        [sds((NQ, 3 * BP, NE), BF16), sds((NF, RT, NE))] + [sds((RT, NS))] * 4,
        [V((NQ, 3 * NB, NE), F32), V((3 * NB, 3 * BP), BF16), V((NQ, NB, NE), F32), V((NF * MP, 3 * BP), BF16)],
        "time",
    )(coef, star, stiffness, proj, halo_send)
    arrived = [shifted(pays[o], SHIFTS[o]) for o in range(4)]
    part, g, wf, idr = call(
        local_kernel,
        [sds((NQ, NB, NE)), sds((NF, RT, NE)), sds((NB, 864), BF16), sds((8, NE), jnp.int32)],
        [
            V((NQ, 3 * NB, NE), F32), V((3 * NB, 3 * BP), BF16), V((NB, 288), BF16),
            V((2, 72, MP), BF16), V((2, 72, MP), BF16), V((NF, RT, NE), F32),
            V((256, 128), F32), V((NF, NE, NE), BF16), V((RT, NE), F32),
        ],
        "local",
    )(coef, xs, tr, star, stiffness, proj, rotation, own_flux, neighbour_slot, neighbour_code, fault_table, params)
    out = call(
        far_kernel,
        sds((NQ, NB, NE)),
        [V((NF, RT, NE), F32), V((NQ, NF * MP, NE), F32), V((3, NF * MP, NE), F32)],
        "far",
    )(part, g, wf, idr, neighbour_flux, neighbour_code, *arrived)
    return jnp.transpose(out, (1, 0, 2))


def solution(mesh):
    e3, e4 = P(None, None, "dom"), P(None, None, None, "dom")
    row = P(None, "dom")
    placed = (e3, e4, e4, e4, P(), P(), P(), e3, e3, P("dom"), row, row, row, row)
    return jax.shard_map(shards, mesh=mesh, in_specs=placed, out_specs=e3, check_vma=False)
```

```python
import functools
import jax
import jax.numpy as jnp
from jax import lax
from jax.experimental import pallas as pl
from jax.experimental.pallas import tpu as pltpu
from jax.sharding import PartitionSpec as P


ORDER = 6
SHIFTS = (1, 2, -1, -2)
F32 = jnp.float32
BF16 = jnp.bfloat16

NB, NQ, NM, NF, NE, NS = 56, 9, 21, 4, 256, 128
MP = 24
BP = 64
RT = NQ * MP
ETA_ROW = 176
PLUS_ROW = 88
GROUPS = ((0, 16), (16, 16), (32, 24))
QL = NQ * 128


def split(x):
    hi = x.astype(BF16)
    lo = (x - hi.astype(F32)).astype(BF16)
    return hi, lo


def dot(a, b):
    return jnp.dot(a, b, preferred_element_type=F32)


def dot_t(a, b):
    return lax.dot_general(a, b, (((1,), (1,)), ((), ())), preferred_element_type=F32)


def put_weights(ref, rows, w, width):
    hi, lo = split(w)
    k = w.shape[1]
    ref[rows, 0:k] = hi
    ref[rows, width : width + k] = lo
    ref[rows, 2 * width : 2 * width + k] = hi


def put_split(ref, q, row, count, x):
    hi, lo = split(x)
    ref[row : row + count, q * 128 : (q + 1) * 128] = hi
    ref[BP + row : BP + row + count, q * 128 : (q + 1) * 128] = lo


def doubled(ref):
    return jnp.concatenate([ref[0:BP], ref[0:BP], ref[BP : 2 * BP]], 0)


def mix_star(t_ref, star_ref, row, count, lanes):
    acc = [None] * NQ
    for p in range(NQ):
        for i in range(3):
            t = t_ref[i * NB + row : i * NB + row + count, p * 128 : (p + 1) * 128]
            for q in range(NQ):
                s = jnp.broadcast_to(star_ref[p, q, i : i + 1, lanes], (count, 128))
                acc[q] = t * s if acc[q] is None else acc[q] + t * s
    return acc


def mix_flux(src_ref, flux_ref, face, lanes):
    acc = [None] * NQ
    for p in range(NQ):
        t = src_ref[face, p * MP : (p + 1) * MP, lanes]
        for q in range(NQ):
            s = jnp.broadcast_to(flux_ref[p, q, face : face + 1, lanes], (MP, 128))
            acc[q] = t * s if acc[q] is None else acc[q] + t * s
    return acc


def one_by_one(count, step):
    def body(i, c):
        for j in range(count):
            pl.when(i == j)(functools.partial(step, j, i))
        return c

    lax.fori_loop(0, count, body, 0)


HALVES = (slice(0, 128), slice(128, 256))


def put_iota(ref):
    ref[...] = lax.broadcasted_iota(jnp.int32, ref.shape, 0).astype(F32).astype(BF16)


def put_one_hot(ref, ids, iota_ref, faces):
    one, zero = jnp.ones((), BF16), jnp.zeros((), BF16)
    for s in range(faces):
        at = ids - s * NE
        at = jnp.where((at >= 0) & (at < NE), at, -1).astype(F32).astype(BF16)
        ref[s * NE : (s + 1) * NE, :] = jnp.where(
            iota_ref[...] == jnp.broadcast_to(at, (NE, NE)), one, zero
        )


def named(names, refs):
    return dict(zip(names, refs))


class Copies:
    def __init__(self, sems):
        self.sems, self.count, self.open = sems, 0, {}

    def made(self, a, b, at, number):
        if at is not None:
            a, b = a.at[at], b.at[at]
        return pltpu.make_async_copy(a, b, self.sems.at[number])

    def reserve(self, names, a, b):
        first = self.count
        for i, name in enumerate(names):
            self.open[name] = (a, b, i, first + i)
        self.count += len(names)
        return lambda i: self.made(a, b, i, first + i).start()

    def start(self, name, a, b, at=None):
        self.open[name] = (a, b, at, self.count)
        self.count += 1
        self.made(*self.open[name]).start()

    def wait(self, *names):
        for name in names:
            self.made(*self.open.pop(name)).wait()

    def finish(self):
        for one in self.open.values():
            self.made(*one).wait()


FIRST_IN = ("stiff", "proj", "coef", "star", "minus", "plus", "eta", "send")
FIRST_OUT = ("packed", "xs0", "xs1", "tr", "th", "tl", "p0", "p1", "p2", "p3")
FIRST_TMP = ("t0", "t1", "w", "int", "pw", "hot", "hot2", "iota", "scr")
FIRST_COPIES = 8 + 6 + 4 + 4


def first_kernel(*refs):
    ni, no = len(FIRST_IN), len(FIRST_OUT)
    hbm = named(FIRST_IN + FIRST_OUT, refs[: ni + no])
    v = named(FIRST_IN + FIRST_OUT, refs[ni + no : 2 * (ni + no)])
    t = named(FIRST_TMP, refs[2 * (ni + no) : -1])
    copies = Copies(refs[-1])
    for name in FIRST_IN:
        copies.start(name, hbm[name], v[name])

    def send(name, *at):
        copies.start((name, at), v[name], hbm[name], *at)

    xs, ts, star_ref, int_ref = (v["xs0"], v["xs1"]), (t["t0"], t["t1"]), v["star"], t["int"]
    w_ref, pw_ref, iota_ref, scr = t["w"], t["pw"], t["iota"], t["scr"]
    w_ref[...] = jnp.zeros_like(w_ref)
    pw_ref[...] = jnp.zeros_like(pw_ref)
    scr[...] = jnp.zeros_like(scr)
    put_iota(iota_ref)
    for x in xs:
        for part in range(2):
            x[part * BP + NB : (part + 1) * BP, :] = jnp.zeros((BP - NB, QL), BF16)
    copies.wait("stiff", "proj")
    for i in range(3):
        put_weights(w_ref, slice(i * NB, (i + 1) * NB), v["stiff"][i], BP)
    for f in range(NF):
        put_weights(pw_ref, slice(f * MP, f * MP + NM), v["proj"][:, f, :], BP)
    copies.wait("coef", "star")

    def start(q, c):
        for h in range(2):
            at = pl.ds(pl.multiple_of(q * 128, 128), 128)
            x = v["coef"][q, :, HALVES[h]]
            int_ref[q, :, HALVES[h]] = x
            hi, lo = split(x)
            xs[h][0:NB, at] = hi
            xs[h][BP : BP + NB, at] = lo
        return c

    lax.fori_loop(0, NQ, start, 0)
    copies.wait("minus", "plus", "eta")
    for p in range(NQ):
        scr[p * NQ : (p + 1) * NQ, :] = v["minus"][p]
        scr[PLUS_ROW + p * NQ : PLUS_ROW + (p + 1) * NQ, :] = v["plus"][p]
    scr[ETA_ROW : ETA_ROW + 1, :] = v["eta"][...]
    v["packed"][:, 0, :] = scr[0:128, :].T
    v["packed"][:, 1, :] = scr[128:256, :].T
    send("packed")
    ts[0][...] = dot(w_ref[...], doubled(xs[0]))

    def mixed(h, factor):
        for row, count in GROUPS:
            acc = mix_star(ts[h], star_ref, row, count, HALVES[h])
            for q in range(NQ):
                put_split(xs[h], q, row, count, acc[q])
                int_ref[q, row : row + count, HALVES[h]] += factor * acc[q]

    def stage(k, factor):
        factor = factor / (k + 2).astype(F32)

        @pl.when(k >= 0)
        def _():
            ts[1][...] = dot(w_ref[...], doubled(xs[1]))
            mixed(0, factor)

        @pl.when(k < ORDER)
        def _():
            ts[0][...] = dot(w_ref[...], doubled(xs[0]))
            mixed(1, factor)

        return factor

    lax.fori_loop(0, ORDER - 1, stage, jnp.float32(1.0))

    def finish(q, c):
        for h in range(2):
            at = pl.ds(pl.multiple_of(q * 128, 128), 128)
            hi, lo = split(int_ref[q, :, HALVES[h]])
            xs[h][0:NB, at] = hi
            xs[h][BP : BP + NB, at] = lo
        return c

    lax.fori_loop(0, NQ, finish, 0)
    send("xs0")
    send("xs1")
    th_ref, tl_ref, tr_ref = v["th"], v["tl"], v["tr"]
    for h in range(2):
        tall = ts[h]
        tall[0 : NF * MP, :] = dot(pw_ref[...], doubled(xs[h]))
    for f in range(NF):
        for h in range(2):
            x = jnp.concatenate(
                [ts[h][f * MP : (f + 1) * MP, q * 128 : (q + 1) * 128] for q in range(NQ)], 0
            )
            tr_ref[f, :, HALVES[h]] = x
            hi, lo = split(x)
            at = slice(f * NE + h * 128, f * NE + (h + 1) * 128)
            th_ref[:, at] = hi
            tl_ref[:, at] = lo

    def picked(hot):
        return dot(th_ref[...], hot[...]) + dot(tl_ref[...], hot[...])

    copies.wait("send")
    for name in ("th", "tl", "tr"):
        send(name)
    for o in range(0, NF, 2):
        send_ref = v["send"]
        ids = jnp.concatenate([send_ref[o : o + 1, :], send_ref[o + 1 : o + 2, :]], 1)
        hot = t["hot"] if o == 0 else t["hot2"]
        put_one_hot(hot, ids, iota_ref, NF)
        got = picked(hot)
        v[f"p{o}"][...] = got[:, :NS]
        v[f"p{o + 1}"][...] = got[:, NS:]
        send(f"p{o}")
        send(f"p{o + 1}")
    copies.finish()


NEAR_IN = ("stiff", "proj", "xs0", "xs1", "star", "coef", "table", "slot", "code", "rot", "th", "tl", "tr", "own")
NEAR_OUT = ("part", "g", "pair", "wf", "pt", "rtw", "idr")
NEAR_TMP = ("t0", "t1", "wv", "hot", "iota", "st", "fhot", "raw", "free", "ids", "rw")
NEAR_COPIES = 14 + 6 + 4


def near_kernel(*refs):
    ni, no = len(NEAR_IN), len(NEAR_OUT)
    hbm = named(NEAR_IN + NEAR_OUT, refs[: ni + no])
    v = named(NEAR_IN + NEAR_OUT, refs[ni + no : 2 * (ni + no)])
    t = named(NEAR_TMP, refs[2 * (ni + no) : -1])
    copies = Copies(refs[-1])
    for name in NEAR_IN:
        copies.start(name, hbm[name], v[name])

    def send(name, *at):
        copies.start((name, at), v[name], hbm[name], *at)

    xs, ts, star_ref = (v["xs0"], v["xs1"]), (t["t0"], t["t1"]), v["star"]
    wv_ref, iota_ref, pt_ref, part_ref = t["wv"], t["iota"], v["pt"], v["part"]
    th_ref, tl_ref, tr_ref, hot_ref = v["th"], v["tl"], v["tr"], t["hot"]
    wv_ref[...] = jnp.zeros_like(wv_ref)
    pt_ref[...] = jnp.zeros_like(pt_ref)
    put_iota(iota_ref)
    copies.wait("stiff", "proj")
    for i in range(3):
        put_weights(wv_ref, slice(i * NB, (i + 1) * NB), v["stiff"][i].T, BP)
    for f in range(NF):
        hi, lo = split(v["proj"][:, f, :].T)
        pt_ref[:, f * MP : f * MP + NM] = hi
        pt_ref[:, 96 + f * MP : 96 + f * MP + NM] = lo
        pt_ref[:, 192 + f * MP : 192 + f * MP + NM] = hi
    send("pt")

    def volume(h, i):
        if h == 0:
            ts[1][...] = dot(wv_ref[...], doubled(xs[1]))
        for row, count in GROUPS:
            acc = mix_star(ts[h], star_ref, row, count, HALVES[h])
            for q in range(NQ):
                x = v["coef"][q, row : row + count, HALVES[h]]
                part_ref[q, row : row + count, HALVES[h]] = x + acc[q]

    copies.wait("xs0", "xs1")
    ts[0][...] = dot(wv_ref[...], doubled(xs[0]))
    copies.wait("star", "coef")
    one_by_one(2, volume)

    def picked(hot):
        return dot(th_ref[...], hot[...]) + dot(tl_ref[...], hot[...])

    copies.wait("table", "slot", "code", "th", "tl", "tr", "own")
    table = v["table"][...]
    active = table[0:1] >= 0
    ids = jnp.concatenate([jnp.where(active, table[0:1], -1), jnp.where(active, table[1:2], -1)], 1)
    turn = table[2:3]
    fhot_ref = t["fhot"]
    put_one_hot(fhot_ref, ids, iota_ref, NF)
    code, slots = v["code"][...], v["slot"][...]
    v["idr"][...] = jnp.full_like(v["idr"], -1)
    ones = jnp.ones((16, NE), BF16)
    for f in range(NF):
        listed = dot_t(ones, fhot_ref[f * NE : (f + 1) * NE, :])[0:1] > 0.5
        t["free"][f : f + 1, :] = jnp.where(listed, 0.0, 1.0)
        slot = slots[f : f + 1]
        remote = slot >= NE
        v["idr"][f : f + 1, :] = jnp.where(remote & ~listed, slot - NE, -1)
        own_id = (code[f : f + 1] // 3) * NE + slot
        t["ids"][f : f + 1, :] = jnp.where(remote | listed, -1, own_id)
    send("idr")
    send_face = copies.reserve([("g", f) for f in range(NF)], v["g"], hbm["g"])

    def by_face(f, i):
        put_one_hot(hot_ref, t["ids"][f : f + 1, :], iota_ref, NF)
        v["g"][f] = picked(hot_ref)
        for h in range(2):
            acc = mix_flux(tr_ref, v["own"], f, HALVES[h])
            keep = t["free"][f : f + 1, HALVES[h]]
            for q in range(NQ):
                t["st"][f, q * MP : (q + 1) * MP, HALVES[h]] = keep * acc[q]

        send_face(i)

    one_by_one(NF, by_face)


    for q in range(NQ):
        rows = slice(q * MP, (q + 1) * MP)
        state = jnp.concatenate([t["st"][f, rows, :] for f in range(NF)], 0)
        hi, lo = split(state)
        part_ref[q] = part_ref[q] - dot(pt_ref[...], jnp.concatenate([hi, hi, lo], 0))
    send("part")
    wf_ref, rw_ref, rtw_ref = v["wf"], t["rw"], v["rtw"]
    copies.wait("rot")
    wf_ref[...] = jnp.zeros_like(wf_ref)
    rw_ref[...] = jnp.zeros_like(rw_ref)
    rtw_ref[...] = jnp.zeros_like(rtw_ref)
    rots = [split(v["rot"][h]) for h in range(3)]
    for h in range(3):
        rw_ref[0, h * MP : h * MP + NM, 0:NM] = rots[h][0]
        rw_ref[1, h * MP : h * MP + NM, 0:NM] = rots[h][1]
        hi, lo = split(v["rot"][h].T)
        rtw_ref[0, h * MP : h * MP + NM, 0:NM] = hi
        rtw_ref[1, h * MP : h * MP + NM, 0:NM] = lo
    for f in range(NF):
        turn_over = v["proj"][:, f, :].T
        hi, lo = split(turn_over)
        for h in range(3):
            rhi, rlo = rots[h]
            whi, wlo = split(dot(hi, rhi) + dot(lo, rhi) + dot(hi, rlo))
            at = h * 96 + f * MP
            wf_ref[:, at : at + NM] = whi
            wf_ref[:, 288 + at : 288 + at + NM] = wlo
            wf_ref[:, 576 + at : 576 + at + NM] = whi
    send("wf")
    send("rtw")
    t["raw"][...] = picked(fhot_ref)
    raw = jnp.concatenate([t["raw"][q * MP : (q + 1) * MP, NS:] for q in range(NQ)], 1)
    ts[0][0:72, :] = turned(rw_ref, raw)
    for q in range(NQ):
        rows = slice(q * MP, (q + 1) * MP)
        v["pair"][rows, :NS] = t["raw"][rows, :NS]
        v["pair"][rows, NS:] = choose(ts[0], turn, q)
    send("pair")
    copies.finish()


def turned(w_ref, x):
    hi, lo = split(x)
    return dot(w_ref[0], hi) + dot(w_ref[1], hi) + dot(w_ref[0], lo)


def choose(ref, turn, q):
    out = jnp.zeros((MP, NS), F32)
    for h in range(3):
        piece = ref[h * MP : (h + 1) * MP, q * NS : (q + 1) * NS]
        out = jnp.where(turn == h, piece, out)
    return out


FAR_IN = ("table", "code", "idr", "params", "rtw", "pair", "pt", "r0", "r1", "r2", "r3", "flux", "g", "wf", "part")
FAR_TMP = ("gs", "z", "mask", "hot", "ehot", "iota", "ph", "pl", "scr", "fs", "back", "lift")
FAR_COPIES = 14 + NF + NQ


def far_kernel(*refs):
    ni = len(FAR_IN)
    hbm = named(FAR_IN + ("out",), refs[: ni + 1])
    v = named(FAR_IN + ("out",), refs[ni + 1 : 2 * ni + 2])
    t = named(FAR_TMP, refs[2 * ni + 2 : -1])
    copies = Copies(refs[-1])
    for name in FAR_IN:
        if name != "g":
            copies.start(name, hbm[name], v[name])
    first = copies.count
    copies.count += NF

    def g_copy(i):
        return copies.made(hbm["g"], v["g"], i, first + i)

    for f in range(NF):
        g_copy(f).start()
    iota_ref = t["iota"]
    put_iota(iota_ref)
    copies.wait("table")
    table = v["table"][...]
    active = table[0:1] >= 0
    ids = jnp.concatenate([jnp.where(active, table[0:1], -1), jnp.where(active, table[1:2], -1)], 1)
    turn = table[2:3]
    copies.wait("code", "idr")
    code = v["code"][...] % 3
    for h in range(3):
        rows = [
            jnp.broadcast_to(jnp.where(code[f : f + 1] == h, 1.0, 0.0), (MP, NE))
            for f in range(NF)
        ]
        t["mask"][h] = jnp.concatenate(rows, 0).astype(BF16)
    copies.wait("params", "rtw", "pair", "pt")
    scr, pair, fs = t["scr"], v["pair"], t["fs"]
    scr[0:128, :] = v["params"][:, 0, :].T
    scr[128:256, :] = v["params"][:, 1, :].T
    eta = scr[ETA_ROW : ETA_ROW + 1, :]
    ratio = eta / (1.0 + eta)

    def param(row):
        return jnp.broadcast_to(scr[pl.ds(row, 1), :], (MP, NS))

    def by_quantity(q, c):
        a = b = None
        for p in range(NQ):
            g, hh = param(p * NQ + q), param(PLUS_ROW + p * NQ + q)
            near = pair[p * MP : (p + 1) * MP, :NS]
            far = pair[p * MP : (p + 1) * MP, NS:]
            x = near * g + far * hh
            y = far * g + near * hh
            a = x if a is None else a + x
            b = y if b is None else b + y
        rows = pl.ds(pl.multiple_of(q * MP, 8), MP)
        slip = jnp.where(q >= 3, ratio, 0.0) * (pair[rows, NS:] - pair[rows, :NS])
        fs[rows, :NS] = a + slip
        fs[rows, NS:] = b - slip
        return c

    lax.fori_loop(0, NQ, by_quantity, 0)
    raw = jnp.concatenate([fs[q * MP : (q + 1) * MP, NS:] for q in range(NQ)], 1)
    t["back"][...] = turned(v["rtw"], raw)
    for q in range(NQ):
        fs[q * MP : (q + 1) * MP, NS:] = choose(t["back"], turn, q)
    face = ids >> 8
    for q in range(NQ):
        x = fs[q * MP : (q + 1) * MP, :]
        tall = jnp.concatenate([jnp.where(face == f, x, 0.0) for f in range(NF)], 0)
        hi, lo = split(tall)
        t["lift"][q * NB : (q + 1) * NB, :] = dot(v["pt"][...], jnp.concatenate([hi, hi, lo], 0))
    ehot_ref = t["ehot"]
    put_one_hot(ehot_ref, jnp.where(ids >= 0, ids & (NE - 1), -1), iota_ref, 1)
    hi, lo = split(t["lift"][...])
    hot = ehot_ref[...]
    t["lift"][...] = dot_t(hi, hot) + dot_t(lo, hot)
    hot_ref = t["hot"]
    copies.wait("r0", "r1", "r2", "r3")
    ph_ref, pl_ref = t["ph"], t["pl"]
    for o in range(NF):
        hi, lo = split(v[f"r{o}"][...])
        ph_ref[:, o * NS : (o + 1) * NS] = hi
        pl_ref[:, o * NS : (o + 1) * NS] = lo
    copies.wait("flux")
    gs_ref = t["gs"]

    def by_face(f, i):
        put_one_hot(hot_ref, v["idr"][f : f + 1, :], iota_ref, 2)
        g_copy(i).wait()
        gs_ref[f] = v["g"][f] + dot(ph_ref[...], hot_ref[...]) + dot(pl_ref[...], hot_ref[...])
        for h in range(2):
            acc = mix_flux(gs_ref, v["flux"], f, HALVES[h])
            for q in range(NQ):
                t["z"][q, f * MP : (f + 1) * MP, HALVES[h]] = acc[q]

    one_by_one(NF, by_face)
    copies.wait("wf", "part")
    send_quantity = copies.reserve([("out", q) for q in range(NQ)], v["out"], hbm["out"])

    def by_quantity(part, i):
        for q in range(3 * part, 3 * part + 3):
            hi, lo = split(t["z"][q])
            his = [hi * t["mask"][h] for h in range(3)]
            los = [lo * t["mask"][h] for h in range(3)]
            lifted = dot(v["wf"][...], jnp.concatenate(his + his + los, 0))
            v["out"][q] = v["part"][q] - t["lift"][q * NB : (q + 1) * NB, :] - lifted
            send_quantity(3 * i + q - 3 * part)

    one_by_one(3, by_quantity)
    copies.finish()


def sds(shape, dtype=F32):
    return jax.ShapeDtypeStruct(shape, dtype)


def shifted(block, distance):
    n = lax.axis_size("dom")
    return lax.ppermute(block, "dom", [((i - distance) % n, i) for i in range(n)])


V = pltpu.VMEM
VMEM_LIMIT = 67043328
IN_HBM = pl.BlockSpec(memory_space=pl.ANY)
DMA = pltpu.SemaphoreType.DMA


def held(arrays):
    return [V(a.shape, a.dtype) for a in arrays]


def call(kernel, ins, out, scratch):
    return pl.pallas_call(
        kernel,
        out_shape=out,
        in_specs=[IN_HBM] * len(ins),
        out_specs=[IN_HBM] * len(out),
        scratch_shapes=scratch,
        compiler_params=pltpu.CompilerParams(vmem_limit_bytes=VMEM_LIMIT),
        cost_estimate=pl.CostEstimate(flops=10**8, bytes_accessed=3 * 10**6, transcendentals=0),
    )(*ins)


def shards(
    coefficients, star_matrices, own_flux, neighbour_flux, stiffness, projection, rotation,
    fault_minus, fault_plus, slip_compliance, neighbour_slot, neighbour_code, halo_send, fault_table,
):
    coef = jnp.transpose(coefficients, (1, 0, 2))
    star = jnp.transpose(star_matrices, (1, 2, 0, 3))
    proj = jnp.transpose(projection, (1, 0, 2))
    t_half = V((3 * NB, QL), F32)
    w_stiff = V((3 * NB, 3 * BP), BF16)
    iota = V((NE, NE), BF16)
    hot = V((NF * NE, NE), BF16)
    flat = V((RT, NF * NE), BF16)
    turn = (2, 72, MP)
    eta = slip_compliance.reshape(1, -1)
    ins = [stiffness, proj, coef, star, fault_minus, fault_plus, eta, halo_send]
    outs = [
        sds((128, 2, 128)), *[sds((2 * BP, QL), BF16)] * 2, sds((NF, RT, NE)),
        *[sds((RT, NF * NE), BF16)] * 2, *[sds((RT, NS))] * 4,
    ]
    packed, xs0, xs1, tr, th, tl, *pays = call(
        first_kernel, ins, outs,
        [
            *held(ins), *held(outs), t_half, t_half, w_stiff, V((NQ, NB, NE), F32),
            V((NF * MP, 3 * BP), BF16), hot, hot, iota, V((256, 128), F32),
            DMA((FIRST_COPIES,)),
        ],
    )
    params = lax.all_to_all(packed, "dom", 0, 0, tiled=True)
    arrived = []
    for o in range(4):
        arrived.append(shifted(pays[o], SHIFTS[o]))
    ins = [
        stiffness, proj, xs0, xs1, star, coef, fault_table, neighbour_slot, neighbour_code,
        rotation, th, tl, tr, own_flux,
    ]
    outs = [
        sds((NQ, NB, NE)), sds((NF, RT, NE)), sds((RT, NE)), sds((NB, 864), BF16),
        sds((NB, 288), BF16), sds(turn, BF16), sds((8, NE), jnp.int32),
    ]
    part, g, pair, wf, pt, rtw, idr = call(
        near_kernel, ins, outs,
        [
            *held(ins), *held(outs), t_half, t_half, w_stiff, hot, iota,
            V((NF, RT, NE), F32), hot, V((RT, NE), F32), V((8, NE), F32),
            V((8, NE), jnp.int32), V(turn, BF16), DMA((NEAR_COPIES,)),
        ],
    )
    ins = [
        fault_table, neighbour_code, idr, params, rtw, pair, pt, *arrived, neighbour_flux, g, wf, part
    ]
    outs = [sds((NQ, NB, NE))]
    (out,) = call(
        far_kernel, ins, outs,
        [
            *held(ins), *held(outs),
            V((NF, RT, NE), F32), V((NQ, NF * MP, NE), F32), V((3, NF * MP, NE), BF16),
            V((2 * NE, NE), BF16), V((NE, NE), BF16), iota, V((RT, 4 * NS), BF16),
            V((RT, 4 * NS), BF16), V((256, 128), F32), V((RT, NE), F32), V((72, QL), F32),
            V((NQ * NB, NE), F32), DMA((FAR_COPIES,)),
        ],
    )
    return jnp.transpose(out, (1, 0, 2))


def solution(mesh):
    e3, e4 = P(None, None, "dom"), P(None, None, None, "dom")
    row = P(None, "dom")
    placed = (e3, e4, e4, e4, P(), P(), P(), e3, e3, P("dom"), row, row, row, row)
    return jax.shard_map(shards, mesh=mesh, in_specs=placed, out_specs=e3, check_vma=False)
```

```python
import functools
import jax
import jax.numpy as jnp
from jax import lax
from jax.experimental import pallas as pl
from jax.experimental.pallas import tpu as pltpu
from jax.sharding import PartitionSpec as P


ORDER = 6
SHIFTS = (1, 2, -1, -2)
F32 = jnp.float32
BF16 = jnp.bfloat16

NB, NQ, NM, NF, NE, NS = 56, 9, 21, 4, 256, 128
MP = 24
BP = 64
RT = NQ * MP
ETA_ROW = 176
PLUS_ROW = 88
GROUPS = ((0, 16), (16, 16), (32, 24))
QL = NQ * 128


def split(x):
    hi = x.astype(BF16)
    lo = (x - hi.astype(F32)).astype(BF16)
    return hi, lo


def dot(a, b):
    return jnp.dot(a, b, preferred_element_type=F32)


def dot_t(a, b):
    return lax.dot_general(a, b, (((1,), (1,)), ((), ())), preferred_element_type=F32)


def put_weights(ref, rows, w, width):
    hi, lo = split(w)
    k = w.shape[1]
    ref[rows, 0:k] = hi
    ref[rows, width : width + k] = lo
    ref[rows, 2 * width : 2 * width + k] = hi


def put_split(ref, q, row, count, x):
    hi, lo = split(x)
    ref[row : row + count, q * 128 : (q + 1) * 128] = hi
    ref[BP + row : BP + row + count, q * 128 : (q + 1) * 128] = lo


def doubled(ref):
    return jnp.concatenate([ref[0:BP], ref[0:BP], ref[BP : 2 * BP]], 0)


def mix_star(t_ref, star_ref, row, count, lanes):
    acc = [None] * NQ
    for p in range(NQ):
        for i in range(3):
            t = t_ref[i * NB + row : i * NB + row + count, p * 128 : (p + 1) * 128]
            for q in range(NQ):
                s = jnp.broadcast_to(star_ref[p, q, i : i + 1, lanes], (count, 128))
                acc[q] = t * s if acc[q] is None else acc[q] + t * s
    return acc


def mix_flux(src_ref, flux_ref, face, lanes):
    acc = [None] * NQ
    for p in range(NQ):
        t = src_ref[face, p * MP : (p + 1) * MP, lanes]
        for q in range(NQ):
            s = jnp.broadcast_to(flux_ref[p, q, face : face + 1, lanes], (MP, 128))
            acc[q] = t * s if acc[q] is None else acc[q] + t * s
    return acc


def one_by_one(count, step):
    def body(i, c):
        for j in range(count):
            pl.when(i == j)(functools.partial(step, j, i))
        return c

    lax.fori_loop(0, count, body, 0)


HALVES = (slice(0, 128), slice(128, 256))


def put_iota(ref):
    ref[...] = lax.broadcasted_iota(jnp.int32, ref.shape, 0).astype(F32).astype(BF16)


def put_one_hot(ref, ids, iota_ref, faces):
    one, zero = jnp.ones((), BF16), jnp.zeros((), BF16)
    for s in range(faces):
        at = ids - s * NE
        at = jnp.where((at >= 0) & (at < NE), at, -1).astype(F32).astype(BF16)
        ref[s * NE : (s + 1) * NE, :] = jnp.where(
            iota_ref[...] == jnp.broadcast_to(at, (NE, NE)), one, zero
        )


def named(names, refs):
    return dict(zip(names, refs))


class Copies:
    def __init__(self, sems):
        self.sems, self.count, self.open = sems, 0, {}

    def made(self, a, b, at, number):
        if at is not None:
            a, b = a.at[at], b.at[at]
        return pltpu.make_async_copy(a, b, self.sems.at[number])

    def reserve(self, names, a, b):
        first = self.count
        for i, name in enumerate(names):
            self.open[name] = (a, b, i, first + i)
        self.count += len(names)
        return lambda i: self.made(a, b, i, first + i).start()

    def start(self, name, a, b, at=None):
        self.open[name] = (a, b, at, self.count)
        self.count += 1
        self.made(*self.open[name]).start()

    def wait(self, *names):
        for name in names:
            self.made(*self.open.pop(name)).wait()

    def finish(self):
        for one in self.open.values():
            self.made(*one).wait()


FIRST_IN = ("stiff", "proj", "coef", "star", "minus", "plus", "eta", "send")
FIRST_OUT = ("packed", "xs0", "xs1", "tr", "th", "tl", "p0", "p1", "p2", "p3")
FIRST_TMP = ("t0", "t1", "w", "int", "pw", "hot", "hot2", "iota", "scr")
FIRST_COPIES = 8 + 6 + 4 + 4


def first_kernel(*refs):
    ni, no = len(FIRST_IN), len(FIRST_OUT)
    hbm = named(FIRST_IN + FIRST_OUT, refs[: ni + no])
    v = named(FIRST_IN + FIRST_OUT, refs[ni + no : 2 * (ni + no)])
    t = named(FIRST_TMP, refs[2 * (ni + no) : -1])
    copies = Copies(refs[-1])
    for name in FIRST_IN:
        copies.start(name, hbm[name], v[name])

    def send(name, *at):
        copies.start((name, at), v[name], hbm[name], *at)

    xs, ts, star_ref, int_ref = (v["xs0"], v["xs1"]), (t["t0"], t["t1"]), v["star"], t["int"]
    w_ref, pw_ref, iota_ref, scr = t["w"], t["pw"], t["iota"], t["scr"]
    w_ref[...] = jnp.zeros_like(w_ref)
    pw_ref[...] = jnp.zeros_like(pw_ref)
    scr[...] = jnp.zeros_like(scr)
    put_iota(iota_ref)
    for x in xs:
        for part in range(2):
            x[part * BP + NB : (part + 1) * BP, :] = jnp.zeros((BP - NB, QL), BF16)
    copies.wait("stiff", "proj")
    for i in range(3):
        put_weights(w_ref, slice(i * NB, (i + 1) * NB), v["stiff"][i], BP)
    for f in range(NF):
        put_weights(pw_ref, slice(f * MP, f * MP + NM), v["proj"][:, f, :], BP)
    copies.wait("coef", "star")

    def start(q, c):
        for h in range(2):
            at = pl.ds(pl.multiple_of(q * 128, 128), 128)
            x = v["coef"][q, :, HALVES[h]]
            int_ref[q, :, HALVES[h]] = x
            hi, lo = split(x)
            xs[h][0:NB, at] = hi
            xs[h][BP : BP + NB, at] = lo
        return c

    lax.fori_loop(0, NQ, start, 0)
    copies.wait("minus", "plus", "eta")
    for p in range(NQ):
        scr[p * NQ : (p + 1) * NQ, :] = v["minus"][p]
        scr[PLUS_ROW + p * NQ : PLUS_ROW + (p + 1) * NQ, :] = v["plus"][p]
    scr[ETA_ROW : ETA_ROW + 1, :] = v["eta"][...]
    v["packed"][:, 0, :] = scr[0:128, :].T
    v["packed"][:, 1, :] = scr[128:256, :].T
    send("packed")
    ts[0][...] = dot(w_ref[...], doubled(xs[0]))

    def mixed(h, factor):
        for row, count in GROUPS:
            acc = mix_star(ts[h], star_ref, row, count, HALVES[h])
            for q in range(NQ):
                put_split(xs[h], q, row, count, acc[q])
                int_ref[q, row : row + count, HALVES[h]] += factor * acc[q]

    def stage(k, factor):
        factor = factor / (k + 2).astype(F32)

        @pl.when(k >= 0)
        def _():
            ts[1][...] = dot(w_ref[...], doubled(xs[1]))
            mixed(0, factor)

        @pl.when(k < ORDER)
        def _():
            ts[0][...] = dot(w_ref[...], doubled(xs[0]))
            mixed(1, factor)

        return factor

    lax.fori_loop(0, ORDER - 1, stage, jnp.float32(1.0))

    def finish(q, c):
        for h in range(2):
            at = pl.ds(pl.multiple_of(q * 128, 128), 128)
            hi, lo = split(int_ref[q, :, HALVES[h]])
            xs[h][0:NB, at] = hi
            xs[h][BP : BP + NB, at] = lo
        return c

    lax.fori_loop(0, NQ, finish, 0)
    send("xs0")
    send("xs1")
    th_ref, tl_ref, tr_ref = v["th"], v["tl"], v["tr"]
    for h in range(2):
        tall = ts[h]
        tall[0 : NF * MP, :] = dot(pw_ref[...], doubled(xs[h]))
    for f in range(NF):
        for h in range(2):
            x = jnp.concatenate(
                [ts[h][f * MP : (f + 1) * MP, q * 128 : (q + 1) * 128] for q in range(NQ)], 0
            )
            tr_ref[f, :, HALVES[h]] = x
            hi, lo = split(x)
            at = slice(f * NE + h * 128, f * NE + (h + 1) * 128)
            th_ref[:, at] = hi
            tl_ref[:, at] = lo

    def picked(hot):
        return dot(th_ref[...], hot[...]) + dot(tl_ref[...], hot[...])

    copies.wait("send")
    for name in ("th", "tl", "tr"):
        send(name)
    for o in range(0, NF, 2):
        send_ref = v["send"]
        ids = jnp.concatenate([send_ref[o : o + 1, :], send_ref[o + 1 : o + 2, :]], 1)
        hot = t["hot"] if o == 0 else t["hot2"]
        put_one_hot(hot, ids, iota_ref, NF)
        got = picked(hot)
        v[f"p{o}"][...] = got[:, :NS]
        v[f"p{o + 1}"][...] = got[:, NS:]
        send(f"p{o}")
        send(f"p{o + 1}")
    copies.finish()


NEAR_IN = ("stiff", "proj", "xs0", "xs1", "star", "coef", "table", "slot", "code", "rot", "th", "tl", "tr", "own", "r0", "r1", "r2", "r3", "flux")
NEAR_OUT = ("part", "pair", "pt", "rtw")
NEAR_TMP = ("t0", "t1", "wv", "hot", "iota", "st", "fhot", "raw", "free", "ids", "rw", "wf", "idr", "g", "z", "mask", "rhot", "ph", "pl")
NEAR_COPIES = 19 + 3 + NQ


def near_kernel(*refs):
    ni, no = len(NEAR_IN), len(NEAR_OUT)
    hbm = named(NEAR_IN + NEAR_OUT, refs[: ni + no])
    v = named(NEAR_IN + NEAR_OUT, refs[ni + no : 2 * (ni + no)])
    t = named(NEAR_TMP, refs[2 * (ni + no) : -1])
    copies = Copies(refs[-1])
    for name in NEAR_IN:
        copies.start(name, hbm[name], v[name])

    def send(name, *at):
        copies.start((name, at), v[name], hbm[name], *at)

    xs, ts, star_ref = (v["xs0"], v["xs1"]), (t["t0"], t["t1"]), v["star"]
    wv_ref, iota_ref, pt_ref, part_ref = t["wv"], t["iota"], v["pt"], v["part"]
    th_ref, tl_ref, tr_ref, hot_ref = v["th"], v["tl"], v["tr"], t["hot"]
    wv_ref[...] = jnp.zeros_like(wv_ref)
    pt_ref[...] = jnp.zeros_like(pt_ref)
    put_iota(iota_ref)
    copies.wait("stiff", "proj")
    for i in range(3):
        put_weights(wv_ref, slice(i * NB, (i + 1) * NB), v["stiff"][i].T, BP)
    for f in range(NF):
        hi, lo = split(v["proj"][:, f, :].T)
        pt_ref[:, f * MP : f * MP + NM] = hi
        pt_ref[:, 96 + f * MP : 96 + f * MP + NM] = lo
        pt_ref[:, 192 + f * MP : 192 + f * MP + NM] = hi
    send("pt")

    def volume(h, i):
        if h == 0:
            ts[1][...] = dot(wv_ref[...], doubled(xs[1]))
        for row, count in GROUPS:
            acc = mix_star(ts[h], star_ref, row, count, HALVES[h])
            for q in range(NQ):
                x = v["coef"][q, row : row + count, HALVES[h]]
                part_ref[q, row : row + count, HALVES[h]] = x + acc[q]

    copies.wait("xs0", "xs1")
    ts[0][...] = dot(wv_ref[...], doubled(xs[0]))
    copies.wait("star", "coef")
    one_by_one(2, volume)

    def picked(hot):
        return dot(th_ref[...], hot[...]) + dot(tl_ref[...], hot[...])

    copies.wait("table", "slot", "code", "th", "tl", "tr", "own")
    table = v["table"][...]
    active = table[0:1] >= 0
    ids = jnp.concatenate([jnp.where(active, table[0:1], -1), jnp.where(active, table[1:2], -1)], 1)
    turn = table[2:3]
    fhot_ref = t["fhot"]
    put_one_hot(fhot_ref, ids, iota_ref, NF)
    code, slots = v["code"][...], v["slot"][...]
    ones = jnp.ones((16, NE), BF16)
    for f in range(NF):
        listed = dot_t(ones, fhot_ref[f * NE : (f + 1) * NE, :])[0:1] > 0.5
        t["free"][f : f + 1, :] = jnp.where(listed, 0.0, 1.0)
        slot = slots[f : f + 1]
        remote = slot >= NE
        t["idr"][f : f + 1, :] = jnp.where(remote & ~listed, slot - NE, -1)
        own_id = (code[f : f + 1] // 3) * NE + slot
        t["ids"][f : f + 1, :] = jnp.where(remote | listed, -1, own_id)
    wf_ref, rw_ref, rtw_ref = t["wf"], t["rw"], v["rtw"]
    copies.wait("rot")
    wf_ref[...] = jnp.zeros_like(wf_ref)
    rw_ref[...] = jnp.zeros_like(rw_ref)
    rtw_ref[...] = jnp.zeros_like(rtw_ref)
    rots = [split(v["rot"][h]) for h in range(3)]
    for h in range(3):
        rw_ref[0, h * MP : h * MP + NM, 0:NM] = rots[h][0]
        rw_ref[1, h * MP : h * MP + NM, 0:NM] = rots[h][1]
        hi, lo = split(v["rot"][h].T)
        rtw_ref[0, h * MP : h * MP + NM, 0:NM] = hi
        rtw_ref[1, h * MP : h * MP + NM, 0:NM] = lo
    for f in range(NF):
        turn_over = v["proj"][:, f, :].T
        hi, lo = split(turn_over)
        for h in range(3):
            rhi, rlo = rots[h]
            whi, wlo = split(dot(hi, rhi) + dot(lo, rhi) + dot(hi, rlo))
            at = h * 96 + f * MP
            wf_ref[:, at : at + NM] = whi
            wf_ref[:, 288 + at : 288 + at + NM] = wlo
            wf_ref[:, 576 + at : 576 + at + NM] = whi
    send("rtw")
    t["raw"][...] = picked(fhot_ref)
    raw = jnp.concatenate([t["raw"][q * MP : (q + 1) * MP, NS:] for q in range(NQ)], 1)
    ts[0][0:72, :] = turned(rw_ref, raw)
    for q in range(NQ):
        rows = slice(q * MP, (q + 1) * MP)
        v["pair"][rows, :NS] = t["raw"][rows, :NS]
        v["pair"][rows, NS:] = choose(ts[0], turn, q)
    send("pair")
    copies.wait("r0", "r1", "r2", "r3", "flux")
    ph_ref, pl_ref = t["ph"], t["pl"]
    for o in range(NF):
        hi, lo = split(v[f"r{o}"][...])
        ph_ref[:, o * NS : (o + 1) * NS] = hi
        pl_ref[:, o * NS : (o + 1) * NS] = lo
    way = code % 3
    for h in range(3):
        rows = [
            jnp.broadcast_to(jnp.where(way[f : f + 1] == h, 1.0, 0.0), (MP, NE))
            for f in range(NF)
        ]
        t["mask"][h] = jnp.concatenate(rows, 0).astype(BF16)
    rhot_ref, g_ref = t["rhot"], t["g"]

    def by_face(f, i):
        put_one_hot(hot_ref, t["ids"][f : f + 1, :], iota_ref, NF)
        put_one_hot(rhot_ref, t["idr"][f : f + 1, :], iota_ref, 2)
        for h in range(2):
            acc = mix_flux(tr_ref, v["own"], f, HALVES[h])
            keep = t["free"][f : f + 1, HALVES[h]]
            for q in range(NQ):
                t["st"][f, q * MP : (q + 1) * MP, HALVES[h]] = keep * acc[q]
        here = picked(hot_ref)
        g_ref[f] = here + (dot(ph_ref[...], rhot_ref[...]) + dot(pl_ref[...], rhot_ref[...]))

    def by_far_face(f, i):
        for h in range(2):
            acc = mix_flux(g_ref, v["flux"], f, HALVES[h])
            for q in range(NQ):
                t["z"][q, f * MP : (f + 1) * MP, HALVES[h]] = acc[q]

    one_by_one(NF, by_face)
    one_by_one(NF, by_far_face)
    send_part = copies.reserve([("part", q) for q in range(NQ)], part_ref, hbm["part"])

    def by_quantity(part, i):
        for q in range(3 * part, 3 * part + 3):
            rows = slice(q * MP, (q + 1) * MP)
            state = jnp.concatenate([t["st"][f, rows, :] for f in range(NF)], 0)
            hi, lo = split(state)
            own = dot(pt_ref[...], jnp.concatenate([hi, hi, lo], 0))
            hi, lo = split(t["z"][q])
            his = [hi * t["mask"][h] for h in range(3)]
            los = [lo * t["mask"][h] for h in range(3)]
            far = dot(t["wf"][...], jnp.concatenate(his + his + los, 0))
            part_ref[q] = part_ref[q] - own - far
            send_part(3 * i + q - 3 * part)

    one_by_one(3, by_quantity)
    copies.finish()


def turned(w_ref, x):
    hi, lo = split(x)
    return dot(w_ref[0], hi) + dot(w_ref[1], hi) + dot(w_ref[0], lo)


def choose(ref, turn, q):
    out = jnp.zeros((MP, NS), F32)
    for h in range(3):
        piece = ref[h * MP : (h + 1) * MP, q * NS : (q + 1) * NS]
        out = jnp.where(turn == h, piece, out)
    return out


FAR_IN = ("table", "params", "rtw", "pair", "pt", "part")
FAR_TMP = ("ehot", "iota", "scr", "fs", "back", "lift")
FAR_COPIES = 6 + NQ


def far_kernel(*refs):
    ni = len(FAR_IN)
    hbm = named(FAR_IN + ("out",), refs[: ni + 1])
    v = named(FAR_IN + ("out",), refs[ni + 1 : 2 * ni + 2])
    t = named(FAR_TMP, refs[2 * ni + 2 : -1])
    copies = Copies(refs[-1])
    for name in FAR_IN:
        copies.start(name, hbm[name], v[name])
    iota_ref = t["iota"]
    put_iota(iota_ref)
    copies.wait("table")
    table = v["table"][...]
    active = table[0:1] >= 0
    ids = jnp.concatenate([jnp.where(active, table[0:1], -1), jnp.where(active, table[1:2], -1)], 1)
    turn = table[2:3]
    copies.wait("params", "rtw", "pair", "pt")
    scr, pair, fs = t["scr"], v["pair"], t["fs"]
    scr[0:128, :] = v["params"][:, 0, :].T
    scr[128:256, :] = v["params"][:, 1, :].T
    eta = scr[ETA_ROW : ETA_ROW + 1, :]
    ratio = eta / (1.0 + eta)

    def param(row):
        return jnp.broadcast_to(scr[pl.ds(row, 1), :], (MP, NS))

    def by_quantity(q, c):
        a = b = None
        for p in range(NQ):
            g, hh = param(p * NQ + q), param(PLUS_ROW + p * NQ + q)
            near = pair[p * MP : (p + 1) * MP, :NS]
            far = pair[p * MP : (p + 1) * MP, NS:]
            x = near * g + far * hh
            y = far * g + near * hh
            a = x if a is None else a + x
            b = y if b is None else b + y
        rows = pl.ds(pl.multiple_of(q * MP, 8), MP)
        slip = jnp.where(q >= 3, ratio, 0.0) * (pair[rows, NS:] - pair[rows, :NS])
        fs[rows, :NS] = a + slip
        fs[rows, NS:] = b - slip
        return c

    lax.fori_loop(0, NQ, by_quantity, 0)
    raw = jnp.concatenate([fs[q * MP : (q + 1) * MP, NS:] for q in range(NQ)], 1)
    t["back"][...] = turned(v["rtw"], raw)
    for q in range(NQ):
        fs[q * MP : (q + 1) * MP, NS:] = choose(t["back"], turn, q)
    face = ids >> 8
    for q in range(NQ):
        x = fs[q * MP : (q + 1) * MP, :]
        tall = jnp.concatenate([jnp.where(face == f, x, 0.0) for f in range(NF)], 0)
        hi, lo = split(tall)
        t["lift"][q * NB : (q + 1) * NB, :] = dot(v["pt"][...], jnp.concatenate([hi, hi, lo], 0))
    ehot_ref = t["ehot"]
    put_one_hot(ehot_ref, jnp.where(ids >= 0, ids & (NE - 1), -1), iota_ref, 1)
    hi, lo = split(t["lift"][...])
    hot = ehot_ref[...]
    copies.wait("part")
    for q in range(NQ):
        rows = slice(q * NB, (q + 1) * NB)
        v["out"][q] = v["part"][q] - (dot_t(hi[rows], hot) + dot_t(lo[rows], hot))
        copies.start(("out", q), v["out"], hbm["out"], q)
    copies.finish()


def sds(shape, dtype=F32):
    return jax.ShapeDtypeStruct(shape, dtype)


def shifted(block, distance):
    n = lax.axis_size("dom")
    return lax.ppermute(block, "dom", [((i - distance) % n, i) for i in range(n)])


V = pltpu.VMEM
VMEM_LIMIT = 67043328
IN_HBM = pl.BlockSpec(memory_space=pl.ANY)
DMA = pltpu.SemaphoreType.DMA


def held(arrays):
    return [V(a.shape, a.dtype) for a in arrays]


def call(kernel, ins, out, scratch):
    return pl.pallas_call(
        kernel,
        out_shape=out,
        in_specs=[IN_HBM] * len(ins),
        out_specs=[IN_HBM] * len(out),
        scratch_shapes=scratch,
        compiler_params=pltpu.CompilerParams(vmem_limit_bytes=VMEM_LIMIT),
        cost_estimate=pl.CostEstimate(flops=10**8, bytes_accessed=3 * 10**6, transcendentals=0),
    )(*ins)


def shards(
    coefficients, star_matrices, own_flux, neighbour_flux, stiffness, projection, rotation,
    fault_minus, fault_plus, slip_compliance, neighbour_slot, neighbour_code, halo_send, fault_table,
):
    coef = jnp.transpose(coefficients, (1, 0, 2))
    star = jnp.transpose(star_matrices, (1, 2, 0, 3))
    proj = jnp.transpose(projection, (1, 0, 2))
    t_half = V((3 * NB, QL), F32)
    w_stiff = V((3 * NB, 3 * BP), BF16)
    iota = V((NE, NE), BF16)
    hot = V((NF * NE, NE), BF16)
    flat = V((RT, NF * NE), BF16)
    turn = (2, 72, MP)
    eta = slip_compliance.reshape(1, -1)
    ins = [stiffness, proj, coef, star, fault_minus, fault_plus, eta, halo_send]
    outs = [
        sds((128, 2, 128)), *[sds((2 * BP, QL), BF16)] * 2, sds((NF, RT, NE)),
        *[sds((RT, NF * NE), BF16)] * 2, *[sds((RT, NS))] * 4,
    ]
    packed, xs0, xs1, tr, th, tl, *pays = call(
        first_kernel, ins, outs,
        [
            *held(ins), *held(outs), t_half, t_half, w_stiff, V((NQ, NB, NE), F32),
            V((NF * MP, 3 * BP), BF16), hot, hot, iota, V((256, 128), F32),
            DMA((FIRST_COPIES,)),
        ],
    )
    params = lax.all_to_all(packed, "dom", 0, 0, tiled=True)
    arrived = []
    for o in range(4):
        arrived.append(shifted(pays[o], SHIFTS[o]))
    ins = [
        stiffness, proj, xs0, xs1, star, coef, fault_table, neighbour_slot, neighbour_code,
        rotation, th, tl, tr, own_flux, *arrived, neighbour_flux,
    ]
    outs = [sds((NQ, NB, NE)), sds((RT, NE)), sds((NB, 288), BF16), sds(turn, BF16)]
    part, pair, pt, rtw = call(
        near_kernel, ins, outs,
        [
            *held(ins), *held(outs), t_half, t_half, w_stiff, hot, iota,
            V((NF, RT, NE), F32), hot, V((RT, NE), F32), V((8, NE), F32),
            V((8, NE), jnp.int32), V(turn, BF16), V((NB, 864), BF16),
            V((8, NE), jnp.int32), V((NF, RT, NE), F32), V((NQ, NF * MP, NE), F32),
            V((3, NF * MP, NE), BF16), V((2 * NE, NE), BF16), V((RT, 4 * NS), BF16),
            V((RT, 4 * NS), BF16), DMA((NEAR_COPIES,)),
        ],
    )
    ins = [fault_table, params, rtw, pair, pt, part]
    outs = [sds((NQ, NB, NE))]
    (out,) = call(
        far_kernel, ins, outs,
        [
            *held(ins), *held(outs), V((NE, NE), BF16), iota, V((256, 128), F32),
            V((RT, NE), F32), V((72, QL), F32), V((NQ * NB, NE), F32), DMA((FAR_COPIES,)),
        ],
    )
    return jnp.transpose(out, (1, 0, 2))


def solution(mesh):
    e3, e4 = P(None, None, "dom"), P(None, None, None, "dom")
    row = P(None, "dom")
    placed = (e3, e4, e4, e4, P(), P(), P(), e3, e3, P("dom"), row, row, row, row)
    return jax.shard_map(shards, mesh=mesh, in_specs=placed, out_specs=e3, check_vma=False)
```
